512 devices in a mesh: region: 64 (over z, y), tile: 8 (over x, core).
Axes of the slice: x: 4, y: 8, z: 8, core: 2. Of those that a mesh axis runs over, the one named last changes fastest.
Arguments:
- innovations: float32 [64, 65536], P(None, ('region', 'tile')), may hold values from -6 to 6
- obs_geometry: float32 [3, 65536], P(None, ('region', 'tile')), may hold values from 0 to 35, as said below
- obs_error: float32 [65536], P(('region', 'tile')), may hold values from 0.25 to 1
- tile_owner: int32 [64, 7], P('region'), may hold values from -1 to 7, as said below
Outputs:
- weights: float32 [64, 65536], P(None, ('region', 'tile'))
- residual: float32 [64, 65536], P(None, ('region', 'tile'))
The draws below stay inside these ranges and needn't reach their ends.
Inputs may be any that keep to these rules, and one draw needn't show every extreme that they name: tile_owner[i, k] names the device along tile that computes the tile of regions i and i + k, or is -1 where that pair is not listed. A region lists the offsets 0 to e - 1 for some e of 1 to 7, and i + k is a region for every listed pair. No device owns more than 4 tiles of its region, and some device owns exactly 4. `obs_geometry`: the standard deviations lie between 0.5 and 2. The operator A built from these positions and the listed tiles is symmetric positive definite.
All inputs are finite; a program needn't handle non-finite values.
Results may differ from the reference program's by a relative error of at most 0.0098.
Values may be sent and summed in bfloat16 or wider, within the bound.
A program may use at most 128 MiB of HBM per device.

```python
import math
import jax
import jax.numpy as jnp
from jax import lax

OBS_REG = 1024
COLS = 64
REACH = 7
ITERS = 2
REGIONS = 64
OBS = 65536
N_TILE = 8


def region_layout(key):
    folded = jax.random.fold_in(key, 7311)
    subkeys = jax.random.split(folded, 4)
    drawn = jax.random.randint(subkeys[0], (REGIONS,), 5, REACH + 1)
    drawn = drawn.at[0].set(REACH)
    regions = jnp.arange(REGIONS, dtype=jnp.int32)
    extent = jnp.minimum(drawn, REGIONS - regions)
    return (extent, drawn, subkeys)


def draw_tile_owner(key, part):
    extent, drawn, subkeys = region_layout(key)
    heaviest = jax.random.randint(subkeys[1], (REGIONS,), 0, N_TILE)
    heaviest = heaviest.at[0].set(N_TILE - 1)
    lowest = jnp.maximum(1, extent - 4)
    highest = jnp.minimum(4, extent)
    heavy_count = jax.random.randint(subkeys[2], (REGIONS,), lowest, highest + 1)
    heavy_count = heavy_count.at[0].set(4)
    rotation = jax.random.randint(subkeys[3], (REGIONS,), 0, N_TILE - 1)
    offsets = jnp.arange(REACH, dtype=jnp.int32)[None, :]
    beyond = offsets - heavy_count[:, None]
    others = (heaviest[:, None] + 1 + (beyond + rotation[:, None]) % (N_TILE - 1)) % N_TILE
    owning = jnp.where(offsets < heavy_count[:, None], heaviest[:, None], others)
    return jnp.where(offsets < extent[:, None], owning, -1).astype(jnp.int32)


def draw_obs_geometry(key, part):
    extent, drawn, subkeys = region_layout(key)
    pieces = jax.random.split(jax.random.fold_in(key, 977), 3)
    along_x = jax.random.uniform(pieces[0], (REGIONS, OBS_REG), jnp.float32)
    across_y = jax.random.uniform(pieces[1], (REGIONS, OBS_REG), jnp.float32)
    regions = jnp.arange(REGIONS).astype(jnp.float32)[:, None]
    span_x = 0.5 * drawn.astype(jnp.float32)[:, None] - 1.0
    position_x = 0.5 * regions + along_x * span_x
    position_y = across_y * (OBS_REG / 32.0)
    spread = jax.random.uniform(pieces[2], (REGIONS, OBS_REG), jnp.float32, 0.8, 1.25)
    return jnp.stack([position_x.reshape(-1), position_y.reshape(-1), spread.reshape(-1)]).astype(jnp.float32)


def shard_levels(stream_key, shape, shards, smallest, high):
    loudness = 1.0
    for dim, shards_of in shards:
        steps = jax.random.uniform(jax.random.fold_in(jax.random.fold_in(stream_key, 6), dim), (shards_of,), jnp.float32, smallest / len(shards), high / len(shards))
        loudness = loudness * jnp.repeat(jnp.exp(steps), shape[dim] // shards_of).reshape((-1,) + (1,) * (len(shape) - 1 - dim))
    return loudness


def scatter_about(rng, shape, scale, limit, cuts=(), kind=jnp.bfloat16):
    result = jax.random.normal(rng, shape, jnp.float32) * scale
    if len(cuts) > 0:
        result = shard_levels(rng, shape, cuts, -0.22, 0.18) * result
    return jnp.clip(result, min=-limit, max=limit).astype(kind)


def setup_inputs(seed: int = 0) -> dict:
    splits = jax.random.split(jax.random.key(seed), 5)
    return {
        "innovations": scatter_about(splits[0], (COLS, OBS), 1.0, 6.0, ((1, 512),), jnp.float32),
        "obs_geometry": draw_obs_geometry(jax.random.fold_in(splits[4], 71), 0),
        "obs_error": jnp.clip(jnp.exp(math.log(1.0) - 1.3862944 * jax.random.uniform(splits[2], (OBS,), jnp.float32) ** shard_levels(splits[2], (OBS,), ((0, 512),), -0.2, 0.2)), 0.25, 1.0),
        "tile_owner": draw_tile_owner(jax.random.fold_in(splits[4], 71), 0),
    }


gc_length = 0.5

def gaspari_cohn(distance):
    scaled = distance / gc_length
    bounded = jnp.maximum(scaled, 1.0)
    near_part = (((-0.25 * scaled + 0.5) * scaled + 0.625) * scaled - 5.0 / 3.0) * scaled * scaled + 1.0
    far_part = ((((scaled / 12.0 - 0.5) * scaled + 0.625) * scaled + 5.0 / 3.0) * scaled - 5.0) * scaled + 4.0 - 2.0 / (3.0 * bounded)
    return jnp.where(scaled <= 1.0, near_part, jnp.where(scaled <= 2.0, far_part, 0.0))

def build_tile(home_rows, far_rows):
    across_x = home_rows[0][:, None] - far_rows[0][None, :]
    across_y = home_rows[1][:, None] - far_rows[1][None, :]
    distance = jnp.sqrt(across_x * across_x + across_y * across_y)
    return (home_rows[2][:, None] * far_rows[2][None, :] * gaspari_cohn(distance)).astype(jnp.bfloat16)

def gram_matrix(left_rows, right_rows):
    return jnp.dot(left_rows.astype(jnp.float32), right_rows.T.astype(jnp.float32), precision=lax.Precision.HIGHEST, preferred_element_type=jnp.float32)

def gram_solve(gram_value, target):
    symmetric = 0.5 * (gram_value + gram_value.T)
    factor = jnp.linalg.cholesky(symmetric)
    interim = lax.linalg.triangular_solve(factor, target, left_side=True, lower=True)
    return lax.linalg.triangular_solve(factor, interim, left_side=True, lower=True, transpose_a=True)

def apply_operator(direction, places, obs_error, tile_owner):
    rounded = direction.astype(jnp.bfloat16)
    blocks = jnp.transpose(rounded.reshape(COLS, REGIONS, OBS_REG), (1, 0, 2))

    def region_step(summed, region):
        for offset in range(REACH):
            partner = jnp.minimum(region + offset, REGIONS - 1).astype(jnp.int32)
            listed = tile_owner[region, offset] >= 0

            def add_tile(current, partner=partner, offset=offset):
                tile_block = build_tile(places[region], places[partner])
                to_home = lax.dot_general(blocks[partner].astype(jnp.float32), tile_block.astype(jnp.float32), (((1,), (1,)), ((), ())), preferred_element_type=jnp.float32)
                current = current.at[region].add(to_home)
                if offset > 0:
                    to_partner = jnp.dot(blocks[region].astype(jnp.float32), tile_block.astype(jnp.float32), preferred_element_type=jnp.float32)
                    current = current.at[partner].add(to_partner)
                return current

            def keep_summed(current):
                return current
            summed = lax.cond(listed, add_tile, keep_summed, summed)
        return (summed, None)
    summed, unused = lax.scan(region_step, jnp.zeros((REGIONS, COLS, OBS_REG), jnp.float32), jnp.arange(REGIONS, dtype=jnp.int32))
    coupled = jnp.transpose(summed, (1, 0, 2)).reshape(COLS, OBS)
    return obs_error[None, :] * direction + coupled

def reference(innovations, obs_geometry, obs_error, tile_owner):
    places = jnp.transpose(obs_geometry.reshape(3, REGIONS, OBS_REG), (1, 0, 2))
    weights = jnp.zeros_like(innovations)
    residual = innovations
    direction = innovations
    squares = gram_matrix(residual, residual)
    for iteration in range(ITERS):
        image_block = apply_operator(direction, places, obs_error, tile_owner)
        curvature = gram_matrix(direction, image_block)
        step_size = gram_solve(curvature, squares)
        weights = weights + jnp.dot(step_size.T, direction, precision=lax.Precision.HIGHEST)
        residual = residual - jnp.dot(step_size.T, image_block, precision=lax.Precision.HIGHEST)
        if iteration + 1 < ITERS:
            next_squares = gram_matrix(residual, residual)
            conjugacy = gram_solve(squares, next_squares)
            direction = residual + jnp.dot(conjugacy.T, direction, precision=lax.Precision.HIGHEST)
            squares = next_squares
    return (weights, residual)
```

```python
import functools

import jax
import jax.numpy as jnp
from jax import lax
from jax.experimental import pallas as pl
from jax.experimental.pallas import tpu as pltpu
from jax.sharding import PartitionSpec as P

MESH = pl.DeviceIdType.MESH
F32 = jnp.float32
BF16 = jnp.bfloat16
HI = lax.Precision.HIGHEST
LANES = 128


def dot_nn(a, b):
    return lax.dot_general(a, b, (((1,), (0,)), ((), ())), precision=HI, preferred_element_type=F32)


def dot_nt(a, b):
    return lax.dot_general(a, b, (((1,), (1,)), ((), ())), precision=HI, preferred_element_type=F32)


def eliminate(matrix, target):
    n = matrix.shape[0]
    work = jnp.concatenate([matrix, target], axis=1)
    rows = lax.broadcasted_iota(jnp.int32, (n, 1), 0)
    for k in range(n):
        row = work[k : k + 1, :] * (1.0 / work[k : k + 1, k : k + 1])
        work = jnp.where(rows == k, row, work - work[:, k : k + 1] * row)
    return work[:, n:]


def tile_block(x_far, y_far, s_far, x_home, y_home, s_home):
    dx = x_far - x_home
    dy = y_far - y_home
    square = jnp.maximum(dx * dx + dy * dy, 1e-30)
    inverse = lax.rsqrt(square)
    z = square * inverse
    near = ((((-0.25 * z + 0.5) * z + 0.625) * z) - 5.0 / 3.0) * square + 1.0
    rest = jnp.maximum(2.0 - z, 0.0)
    rest2 = rest * rest
    far = rest2 * rest2 * ((z * (1.0 / 12.0) + 1.0 / 6.0) - inverse * (1.0 / 24.0))
    return (s_far * s_home) * jnp.where(z <= 1.0, near, far)


class Exchange:
    def __init__(self, send_sems, recv_sems, base):
        self.send_sems, self.recv_sems, self.base = send_sems, recv_sems, base

    def copy(self, src, dst, index, device):
        return pltpu.make_async_remote_copy(
            src_ref=src,
            dst_ref=dst,
            send_sem=self.send_sems.at[self.base + index],
            recv_sem=self.recv_sems.at[self.base + index],
            device_id=device,
            device_id_type=MESH,
        )


def kernel(
    cfg, v0_ref, geo_ref, err_ref, own_ref, w_ref, r_ref,
    pb, hb, xb, yb, sb, ub0, ub1, cb, acc0, acc1, rs0, rs1, v1_ref, v2_ref, basis,
    l1, t1, y1, z1, g1, l2, t2, y2, z2, g2, send_sems, recv_sems,
):
    R, T, NY, REACH = cfg
    NZ = R // NY
    S = 2 * REACH - 1
    n = v0_ref.shape[0]
    mid = REACH - 1
    r = lax.axis_index("region")
    t = lax.axis_index("tile")
    y = lax.rem(r, NY)
    z = lax.div(r, NY)
    offsets = [d for k in range(1, REACH) for d in (k, -k)]

    def region(d):
        return (lax.rem(r + d + R, R), t)

    def along_tile(o):
        return (r, lax.rem(t + o, T))

    def along_y(o):
        return (z * NY + lax.rem(y + o, NY), t)

    def along_z(o):
        return (lax.rem(z + o, NZ) * NY + y, t)

    peers = [region(d) for d in offsets] + [along_tile(o) for o in range(1, T)]
    peers += [along_y(o) for o in range(1, NY)] + [along_z(o) for o in range(1, NZ)]

    barrier = pltpu.get_barrier_semaphore()
    for peer in peers:
        pl.semaphore_signal(barrier, inc=1, device_id=peer, device_id_type=MESH)

    base = [0]

    def stage(count):
        made = Exchange(send_sems, recv_sems, base[0])
        base[0] += count
        return made

    pb[mid, 0:2, :] = geo_ref[0:2, :] * 2.0
    pb[mid, 2:3, :] = geo_ref[2:3, :]
    pb[mid, 3:4, :] = jnp.zeros((1, LANES), F32)
    pb[mid, 3:4, 0:REACH] = jnp.where(own_ref[0:1, :] >= 0, 1.0, 0.0)
    pb[mid, 4:8, :] = jnp.zeros((4, LANES), F32)
    hb[0] = pb[mid]
    ub0[mid] = v0_ref[...].astype(BF16)

    pl.semaphore_wait(barrier, len(peers))

    geo_stage, home_stage, u0_stage = stage(len(offsets)), stage(T - 1), stage(len(offsets))
    sends = []
    for index, d in enumerate(offsets):
        sends.append(geo_stage.copy(pb.at[mid], pb.at[mid - d], index, region(d)))
    for o in range(1, T):
        sends.append(home_stage.copy(hb.at[0], hb.at[o], o - 1, along_tile(o)))
    for index, d in enumerate(offsets):
        sends.append(u0_stage.copy(ub0.at[mid], ub0.at[mid - d], index, region(d)))
    for copy in sends:
        copy.start()
    for copy in sends[: len(offsets) + T - 1]:
        copy.wait_recv()

    for s in range(S):
        block = pb[s]
        d = s - mid
        listed = pb[mid if d >= 0 else s, 3:4, abs(d) : abs(d) + 1]
        columns = block.T
        xb[s] = jnp.broadcast_to(columns[:, 0:1], (LANES, LANES))
        yb[s] = jnp.broadcast_to(columns[:, 1:2], (LANES, LANES))
        sb[s] = jnp.broadcast_to(columns[:, 2:3] * listed, (LANES, LANES))

    def build(step, carry):
        for o in range(T):
            home = hb[o]
            block = tile_block(xb[step], yb[step], sb[step], home[0:1, :], home[1:2, :], home[2:3, :])
            cb[o, step] = block.astype(BF16)
        return carry

    lax.fori_loop(0, S, build, 0)

    def apply(ub, acc, rs, v_ref, out_ref):
        found = stage(T - 1)
        whole = jnp.concatenate([ub[s] for s in range(S)], axis=1)

        def out_copy(o):
            return found.copy(acc.at[o], rs.at[o - 1], o - 1, (r, lax.rem(t - o + T, T)))

        def product(step, carry):
            o = lax.rem(step + 1, T)
            acc[o] = jnp.dot(whole, cb[o].reshape(S * LANES, LANES), preferred_element_type=F32)

            @pl.when(step >= 1)
            def _():
                out_copy(step).start()

            return carry

        lax.fori_loop(0, T, product, 0)
        total = err_ref[...] * v_ref[...] + acc[0]
        for o in range(1, T):
            copy = out_copy(o)
            copy.wait_recv()
            total = total + rs[o - 1]
            sends.append(copy)
        out_ref[...] = total

    for copy in sends[len(offsets) + T - 1 :]:
        copy.wait_recv()
    apply(ub0, acc0, rs0, v0_ref, v1_ref)

    ub1[mid] = v1_ref[...].astype(BF16)
    u1_stage = stage(len(offsets))
    u1_copies = [u1_stage.copy(ub1.at[mid], ub1.at[mid - d], index, region(d)) for index, d in enumerate(offsets)]

    class Sum:
        def __init__(self, local, tile_part, y_part, z_part, result):
            self.local, self.parts, self.result = local, (tile_part, y_part, z_part), result
            self.stages = [stage(T - 1), stage(NY - 1), stage(NZ - 1), stage(T - 1)]
            self.pending = []

        def start(self, copies):
            for copy in copies:
                copy.start()
            self.pending = copies
            sends.extend(copies)

        def wait(self):
            for copy in self.pending:
                copy.wait_recv()

        def send_tile(self):
            self.parts[0][t] = self.local[t]
            self.start([
                self.stages[0].copy(self.local.at[lax.rem(t + o, T)], self.parts[0].at[t], o - 1, along_tile(o))
                for o in range(1, T)
            ])

        def total(self, part, count):
            self.wait()
            value = part[0]
            for i in range(1, count):
                value = value + part[i]
            return value

        def send_y(self):
            self.parts[1][y] = self.total(self.parts[0], T)
            part = self.parts[1].at[y]
            self.start([self.stages[1].copy(part, part, o - 1, along_y(o)) for o in range(1, NY)])

        def send_z(self):
            self.parts[2][z] = self.total(self.parts[1], NY)
            part = self.parts[2].at[z]
            self.start([self.stages[2].copy(part, part, o - 1, along_z(o)) for o in range(1, NZ)])

        def send_result(self):
            self.result[t] = self.total(self.parts[2], NZ)
            part = self.result.at[t]
            self.start([self.stages[3].copy(part, part, o - 1, along_tile(o)) for o in range(1, T)])

        def finish(self):
            self.wait()
            return self.result[...].reshape(-1, LANES)

    first = Sum(l1, t1, y1, z1, g1)
    second = Sum(l2, t2, y2, z2, g2)

    for copy in u1_copies:
        copy.start()
        sends.append(copy)
    basis[:n, :LANES] = v0_ref[...]
    basis[n:, :LANES] = v1_ref[...]
    basis[:n, LANES:] = v1_ref[...]
    both = basis[:, :LANES]
    l1[...] = dot_nt(both, both).reshape(l1.shape)
    first.send_tile()
    first.send_y()
    for copy in u1_copies:
        copy.wait_recv()
    apply(ub1, acc1, rs1, v1_ref, v2_ref)
    l2[...] = dot_nt(v2_ref[...], both).reshape(l2.shape)
    second.send_tile()
    first.send_z()
    second.send_y()
    first.send_result()

    v0, v1, v2 = v0_ref[...], v1_ref[...], v2_ref[...]
    gram = first.finish()
    g00, g01, g10, g11 = gram[:n, :n], gram[:n, n:], gram[n:, :n], gram[n:, n:]
    step1 = eliminate(0.5 * (g01 + g01.T), g00)
    next_squares = (g00 - dot_nn(g01, step1)) - dot_nn(step1.T, g10 - dot_nn(g11, step1))
    conjugacy = eliminate(0.5 * (g00 + g00.T), next_squares)
    eye = (
        lax.broadcasted_iota(jnp.int32, (n, n), 0) == lax.broadcasted_iota(jnp.int32, (n, n), 1)
    ).astype(F32)
    p = jnp.concatenate([eye + conjugacy.T, -step1.T], axis=1)
    second.send_z()
    basis[n:, LANES:] = v2
    ahead = dot_nn(p, basis[...])
    moved = dot_nn(step1.T, basis[:n, :])
    on_v1 = dot_nn(p, gram[:, n:])
    second.send_result()
    on_v2 = dot_nt(p, second.finish())
    curvature = dot_nt(jnp.concatenate([on_v1, on_v2], axis=1), p)
    step2 = eliminate(0.5 * (curvature + curvature.T), next_squares).T
    update = dot_nn(step2, ahead)
    w_ref[...] = moved[:, :LANES] + update[:, :LANES]
    r_ref[...] = (v0 - moved[:, LANES:]) - update[:, LANES:]
    for copy in sends:
        copy.wait_send()


def solution(mesh):
    R, T = mesh.shape["region"], mesh.shape["tile"]
    NY = 8 if R % 8 == 0 else 2
    NZ = R // NY

    def shards(innovations, obs_geometry, obs_error, tile_owner):
        n, m = innovations.shape
        reach = tile_owner.shape[1]
        S = 2 * reach - 1
        copies = 3 * 2 * (reach - 1) + 3 * (T - 1) + 2 * (2 * (T - 1) + NY - 1 + NZ - 1)
        h1, h2 = 2 * n // T, n // T

        def buffer(count, rows):
            return pltpu.VMEM((count, rows, LANES), F32)

        def sum_buffers(h):
            return [buffer(T, h), buffer(T, h), buffer(NY, h), buffer(NZ, h), buffer(T, h)]

        return pl.pallas_call(
            functools.partial(kernel, (R, T, NY, reach)),
            out_shape=[jax.ShapeDtypeStruct((n, m), F32)] * 2,
            in_specs=[pl.BlockSpec(memory_space=pltpu.VMEM)] * 4,
            out_specs=[pl.BlockSpec(memory_space=pltpu.VMEM)] * 2,
            scratch_shapes=[
                buffer(S, 8), buffer(T, 8),
                buffer(S, LANES), buffer(S, LANES), buffer(S, LANES),
                pltpu.VMEM((S, n, LANES), BF16), pltpu.VMEM((S, n, LANES), BF16),
                pltpu.VMEM((T, S, LANES, LANES), BF16),
                buffer(T, n), buffer(T, n), buffer(T - 1, n), buffer(T - 1, n),
                pltpu.VMEM((n, LANES), F32), pltpu.VMEM((n, LANES), F32), pltpu.VMEM((2 * n, 2 * LANES), F32),
                *sum_buffers(h1), *sum_buffers(h2),
                pltpu.SemaphoreType.DMA((copies,)), pltpu.SemaphoreType.DMA((copies,)),
            ],
            compiler_params=pltpu.CompilerParams(collective_id=0, has_side_effects=True),
        )(innovations, obs_geometry, obs_error.reshape(1, m), tile_owner)

    return jax.shard_map(
        shards,
        mesh=mesh,
        in_specs=(
            P(None, ("region", "tile")),
            P(None, ("region", "tile")),
            P(("region", "tile")),
            P("region", None),
        ),
        out_specs=(P(None, ("region", "tile")), P(None, ("region", "tile"))),
        check_vma=False,
    )
```

```python
import functools

import jax
import jax.numpy as jnp
from jax import lax
from jax.experimental import pallas as pl
from jax.experimental.pallas import tpu as pltpu
from jax.sharding import PartitionSpec as P

MESH = pl.DeviceIdType.MESH
F32 = jnp.float32
BF16 = jnp.bfloat16
HI = lax.Precision.HIGHEST
LANES = 128


def dot_nn(a, b):
    return lax.dot_general(a, b, (((1,), (0,)), ((), ())), precision=HI, preferred_element_type=F32)


def dot_nt(a, b):
    return lax.dot_general(a, b, (((1,), (1,)), ((), ())), precision=HI, preferred_element_type=F32)


def eliminate(matrix, target):
    n = matrix.shape[0]
    work = jnp.concatenate([matrix, target], axis=1)
    work = work * (1.0 / work[0:1, 0:1])
    rows = lax.broadcasted_iota(jnp.int32, (n, 1), 0)
    for k in range(0, n, 4):
        col = [jnp.broadcast_to(work[:, k + i : k + i + 1], work.shape) for i in range(4)]
        row = [work[k + i : k + i + 1, :] for i in range(4)]

        def at(i, j):
            return col[j][k + i : k + i + 1, :]

        a, b, c = at(0, 0), at(0, 1), at(1, 1)
        e, f, g, h = at(0, 2), at(0, 3), at(1, 2), at(1, 3)
        p, q, s = at(2, 2), at(2, 3), at(3, 3)
        inverse = 1.0 / (a * c - b * b)
        n0, n1 = (c * row[0] - b * row[1]) * inverse, (a * row[1] - b * row[0]) * inverse
        e1, f1 = (c * e - b * g) * inverse, (c * f - b * h) * inverse
        g1, h1 = (a * g - b * e) * inverse, (a * h - b * f) * inverse
        p, q, s = p - (e * e1 + g * g1), q - (e * f1 + g * h1), s - (f * f1 + h * h1)
        r2, r3 = row[2] - (e * n0 + g * n1), row[3] - (f * n0 + h * n1)
        inverse = 1.0 / (p * s - q * q)
        m2, m3 = (s * r2 - q * r3) * inverse, (p * r3 - q * r2) * inverse
        m0, m1 = n0 - (e1 * m2 + f1 * m3), n1 - (g1 * m2 + h1 * m3)
        work = work - (col[0] * m0 + col[1] * m1) - (col[2] * m2 + col[3] * m3)
        for i, solved in enumerate((m0, m1, m2, m3)):
            work = jnp.where(rows == k + i, solved, work)
    return work[:, n:]


def tile_block(x_far, y_far, s_far, x_home, y_home, s_home):
    dx = x_far - x_home
    dy = y_far - y_home
    square = jnp.maximum(dx * dx + dy * dy, 1e-30)
    inverse = lax.rsqrt(square)
    z = square * inverse
    near = ((((-0.25 * z + 0.5) * z + 0.625) * z) - 5.0 / 3.0) * square + 1.0
    rest = jnp.maximum(2.0 - z, 0.0)
    rest2 = rest * rest
    far = rest2 * rest2 * ((z * (1.0 / 12.0) + 1.0 / 6.0) - inverse * (1.0 / 24.0))
    return (s_far * s_home) * jnp.where(z <= 1.0, near, far)


class Exchange:
    def __init__(self, send_sems, recv_sems, base):
        self.send_sems, self.recv_sems, self.base = send_sems, recv_sems, base

    def copy(self, src, dst, index, device):
        return pltpu.make_async_remote_copy(
            src_ref=src,
            dst_ref=dst,
            send_sem=self.send_sems.at[self.base + index],
            recv_sem=self.recv_sems.at[self.base + index],
            device_id=device,
            device_id_type=MESH,
        )


def kernel(
    cfg, v0_ref, geo_ref, err_ref, own_ref, w_ref, r_ref,
    pb, hb, xb, yb, sb, ub0, ub1, cb, acc0, acc1, rs0, rs1, v1_ref, vt, basis,
    l1, t1, y1, z1, g1, l2, t2, y2, z2, g2, send_sems, recv_sems,
):
    R, T, NY, REACH = cfg
    NZ = R // NY
    S = 2 * REACH - 1
    n = v0_ref.shape[0]
    mid = REACH - 1
    r = lax.axis_index("region")
    t = lax.axis_index("tile")
    y = lax.rem(r, NY)
    z = lax.div(r, NY)
    offsets = [d for k in sorted(range(1, REACH), key=lambda k: -min(k, NY - k)) for d in (k, -k)]
    split = REACH // 2 + 1
    far = [i for i, d in enumerate(offsets) if abs(d) >= split]
    near = [i for i, d in enumerate(offsets) if abs(d) < split]
    far_slots = list(range(0, mid - split + 1)) + list(range(mid + split, S))
    near_slots = list(range(mid - split + 1, mid + split))

    def region(d):
        return (lax.rem(r + d + R, R), t)

    def along_tile(o):
        return (r, lax.rem(t + o, T))

    def along_y(o):
        return (z * NY + lax.rem(y + o, NY), t)

    def along_z(o):
        return (lax.rem(z + o, NZ) * NY + y, t)

    peers = [region(d) for d in offsets] + [along_tile(o) for o in range(1, T)]
    peers += [along_y(o) for o in range(1, NY)] + [along_z(o) for o in range(1, NZ)]

    barrier = pltpu.get_barrier_semaphore()
    for peer in peers:
        pl.semaphore_signal(barrier, inc=1, device_id=peer, device_id_type=MESH)

    base = [0]

    def stage(count):
        made = Exchange(send_sems, recv_sems, base[0])
        base[0] += count
        return made

    pb[mid, 0:2, :] = geo_ref[0:2, :] * 2.0
    pb[mid, 2:3, :] = geo_ref[2:3, :]
    pb[mid, 3:4, :] = jnp.zeros((1, LANES), F32)
    pb[mid, 3:4, 0:REACH] = jnp.where(own_ref[0:1, :] >= 0, 1.0, 0.0)
    hb[0] = pb[mid]
    ub0[mid] = v0_ref[...].astype(BF16)
    vt[0, :n] = v0_ref[...]

    pl.semaphore_wait(barrier, len(peers))

    geo_stage, home_stage, u0_stage = stage(len(offsets)), stage(T - 1), stage(len(offsets))
    sends = []
    for index, d in enumerate(offsets):
        sends.append(geo_stage.copy(pb.at[mid], pb.at[mid - d], index, region(d)))
    for o in range(1, T):
        sends.append(home_stage.copy(hb.at[0], hb.at[o], o - 1, along_tile(o)))
    for index, d in enumerate(offsets):
        sends.append(u0_stage.copy(ub0.at[mid], ub0.at[mid - d], index, region(d)))
    begin_stage = stage(T - 1)
    begin_copies = [begin_stage.copy(vt.at[0, :n], vt.at[o, :n], o - 1, along_tile(o)) for o in range(1, T)]
    for copy in sends + begin_copies:
        copy.start()
    for copy in sends[: len(offsets) + T - 1]:
        copy.wait_recv()

    for s in range(S):
        block = pb[s]
        d = s - mid
        listed = pb[mid if d >= 0 else s, 3:4, abs(d) : abs(d) + 1]
        columns = block.T
        xb[s] = jnp.broadcast_to(columns[:, 0:1], (LANES, LANES))
        yb[s] = jnp.broadcast_to(columns[:, 1:2], (LANES, LANES))
        sb[s] = jnp.broadcast_to(columns[:, 2:3] * listed, (LANES, LANES))

    def build(step, carry):
        for o in range(T):
            home = hb[o]
            block = tile_block(xb[step], yb[step], sb[step], home[0:1, :], home[1:2, :], home[2:3, :])
            cb[o, step] = block.astype(BF16)
        return carry

    lax.fori_loop(0, S, build, 0)

    def product(ub, acc, slots, add=False, copies=None):
        whole = jnp.concatenate([ub[s] for s in slots], axis=1)
        low, high = [s for s in slots if s < mid], [s for s in slots if s >= mid]
        runs = [low, high] if low and high and low[-1] + 1 != high[0] else [slots]

        def chunk(step, carry):
            o = lax.rem(step + 1, T)
            tiles = [cb[o, run[0] : run[-1] + 1].reshape(len(run) * LANES, LANES) for run in runs]
            tiles = tiles[0] if len(tiles) == 1 else jnp.concatenate(tiles, axis=0)
            value = jnp.dot(whole, tiles, preferred_element_type=F32)
            acc[o] = acc[o] + value if add else value
            if copies is not None:

                @pl.when(step >= 1)
                def _():
                    copies(step).start()

            return carry

        lax.fori_loop(0, T, chunk, 0)

    def scatter(acc, rs):
        found = stage(T - 1)

        def copies(o):
            return found.copy(acc.at[o], rs.at[o - 1], o - 1, (r, lax.rem(t - o + T, T)))

        return copies

    def gathered(acc, rs, copies):
        total = acc[0]
        for o in range(1, T):
            copy = copies(o)
            copy.wait_recv()
            total = total + rs[o - 1]
            sends.append(copy)
        return total

    for copy in sends[len(offsets) + T - 1 :]:
        copy.wait_recv()
    sends.extend(begin_copies)
    scatter0 = scatter(acc0, rs0)
    product(ub0, acc0, list(range(S)), copies=scatter0)
    v1_ref[...] = err_ref[...] * v0_ref[...] + gathered(acc0, rs0, scatter0)

    ub1[mid] = v1_ref[...].astype(BF16)
    u1_stage = stage(len(offsets))
    u1_copies = [u1_stage.copy(ub1.at[mid], ub1.at[mid - d], index, region(d)) for index, d in enumerate(offsets)]

    class Sum:
        def __init__(self, local, tile_part, y_part, z_part, result):
            self.local, self.parts, self.result = local, (tile_part, y_part, z_part), result
            self.stages = [stage(T - 1), stage(NY - 1), stage(NZ - 1), stage(T - 1)]
            self.pending = []

        def start(self, copies):
            for copy in copies:
                copy.start()
            self.pending = copies
            sends.extend(copies)

        def wait(self):
            for copy in self.pending:
                copy.wait_recv()

        def send_tile(self):
            self.parts[0][t] = self.local[t]
            self.start([
                self.stages[0].copy(self.local.at[lax.rem(t + o, T)], self.parts[0].at[t], o - 1, along_tile(o))
                for o in range(1, T)
            ])

        def total(self, part, count):
            self.wait()
            value = part[0]
            for i in range(1, count):
                value = value + part[i]
            return value

        def send_y(self):
            self.parts[1][y] = self.total(self.parts[0], T)
            part = self.parts[1].at[y]
            self.start([self.stages[1].copy(part, part, o - 1, along_y(o)) for o in range(1, NY)])

        def send_z(self):
            self.parts[2][z] = self.total(self.parts[1], NY)
            part = self.parts[2].at[z]
            self.start([self.stages[2].copy(part, part, o - 1, along_z(o)) for o in range(1, NZ)])

        def send_result(self):
            self.result[t] = self.total(self.parts[2], NZ)
            part = self.result.at[t]
            self.start([self.stages[3].copy(part, part, o - 1, along_tile(o)) for o in range(1, T)])

        def finish(self):
            self.wait()
            return self.result[...].reshape(-1, LANES)

    first = Sum(l1, t1, y1, z1, g1)
    second = Sum(l2, t2, y2, z2, g2)

    for copy in u1_copies:
        copy.start()
    sends.extend(u1_copies)
    vt[0, n:] = v1_ref[...]
    both = vt[0]
    l1[...] = dot_nt(both, both).reshape(l1.shape)
    first.send_tile()
    basis_stage = stage(T - 1)
    basis_copies = [basis_stage.copy(vt.at[0, n:], vt.at[o, n:], o - 1, along_tile(o)) for o in range(1, T)]
    for copy in basis_copies:
        copy.start()
    sends.extend(basis_copies)
    first.send_y()
    for index in far:
        u1_copies[index].wait_recv()
    product(ub1, acc1, far_slots)
    first.send_z()
    for index in near:
        u1_copies[index].wait_recv()
    product(ub1, acc1, near_slots, add=True)
    acc1[0] = acc1[0] + err_ref[...] * v1_ref[...]

    for copy in begin_copies + basis_copies:
        copy.wait_recv()
    part = jnp.concatenate([acc1[o] for o in range(T)], axis=1)
    whole = jnp.concatenate([vt[o] for o in range(T)], axis=1)
    l2[...] = dot_nt(part, whole).reshape(l2.shape)
    second.send_tile()
    scatter1 = scatter(acc1, rs1)
    for o in range(1, T):
        scatter1(o).start()
    first.send_result()
    second.send_y()

    gram = first.finish()
    g00, g01, g10, g11 = gram[:n, :n], gram[:n, n:], gram[n:, :n], gram[n:, n:]
    step1 = eliminate(0.5 * (g01 + g01.T), g00)
    next_squares = (g00 - dot_nn(g01, step1)) - dot_nn(step1.T, g10 - dot_nn(g11, step1))
    second.send_z()
    conjugacy = eliminate(0.5 * (g00 + g00.T), next_squares)
    eye = (
        lax.broadcasted_iota(jnp.int32, (n, n), 0) == lax.broadcasted_iota(jnp.int32, (n, n), 1)
    ).astype(F32)
    p = jnp.concatenate([eye + conjugacy.T, -step1.T], axis=1)
    on_v1 = dot_nn(p, gram[:, n:])
    second.send_result()
    v0, v1 = v0_ref[...], v1_ref[...]
    basis[:n, :LANES] = v0
    basis[n:, :LANES] = v1
    basis[:n, LANES:] = v1
    basis[n:, LANES:] = gathered(acc1, rs1, scatter1)
    ahead = dot_nn(p, basis[...])
    moved = dot_nn(step1.T, basis[:n, :])
    on_v2 = dot_nt(p, second.finish())
    curvature = dot_nt(jnp.concatenate([on_v1, on_v2], axis=1), p)
    step2 = eliminate(0.5 * (curvature + curvature.T), next_squares).T
    update = dot_nn(step2, ahead)
    w_ref[...] = moved[:, :LANES] + update[:, :LANES]
    r_ref[...] = (v0 - moved[:, LANES:]) - update[:, LANES:]
    for copy in sends:
        copy.wait_send()


def solution(mesh):
    R, T = mesh.shape["region"], mesh.shape["tile"]
    NY = 8 if R % 8 == 0 else 2
    NZ = R // NY

    def shards(innovations, obs_geometry, obs_error, tile_owner):
        n, m = innovations.shape
        reach = tile_owner.shape[1]
        S = 2 * reach - 1
        copies = 3 * 2 * (reach - 1) + 5 * (T - 1) + 2 * (2 * (T - 1) + NY - 1 + NZ - 1)
        h1, h2 = 2 * n // T, n // T

        def buffer(count, rows):
            return pltpu.VMEM((count, rows, LANES), F32)

        def sum_buffers(h):
            return [buffer(T, h), buffer(T, h), buffer(NY, h), buffer(NZ, h), buffer(T, h)]

        return pl.pallas_call(
            functools.partial(kernel, (R, T, NY, reach)),
            out_shape=[jax.ShapeDtypeStruct((n, m), F32)] * 2,
            in_specs=[pl.BlockSpec(memory_space=pltpu.VMEM)] * 4,
            out_specs=[pl.BlockSpec(memory_space=pltpu.VMEM)] * 2,
            scratch_shapes=[
                buffer(S, 4), buffer(T, 4),
                buffer(S, LANES), buffer(S, LANES), buffer(S, LANES),
                pltpu.VMEM((S, n, LANES), BF16), pltpu.VMEM((S, n, LANES), BF16),
                pltpu.VMEM((T, S, LANES, LANES), BF16),
                buffer(T, n), buffer(T, n), buffer(T - 1, n), buffer(T - 1, n),
                pltpu.VMEM((n, LANES), F32), buffer(T, 2 * n), pltpu.VMEM((2 * n, 2 * LANES), F32),
                *sum_buffers(h1), *sum_buffers(h2),
                pltpu.SemaphoreType.DMA((copies,)), pltpu.SemaphoreType.DMA((copies,)),
            ],
            compiler_params=pltpu.CompilerParams(collective_id=0, has_side_effects=True),
        )(innovations, obs_geometry, obs_error.reshape(1, m), tile_owner)

    return jax.shard_map(
        shards,
        mesh=mesh,
        in_specs=(
            P(None, ("region", "tile")),
            P(None, ("region", "tile")),
            P(("region", "tile")),
            P("region", None),
        ),
        out_specs=(P(None, ("region", "tile")), P(None, ("region", "tile"))),
        check_vma=False,
    )
```

```python
import functools

import jax
import jax.numpy as jnp
from jax import lax
from jax.experimental import pallas as pl
from jax.experimental.pallas import tpu as pltpu
from jax.sharding import PartitionSpec as P

MESH = pl.DeviceIdType.MESH
F32 = jnp.float32
BF16 = jnp.bfloat16
HI = lax.Precision.HIGHEST
LANES = 128
RELAY = {4: 2, -4: -2, 3: 2, -3: -2, 5: 6, -5: -6}


def dot_nn(a, b):
    return lax.dot_general(a, b, (((1,), (0,)), ((), ())), precision=HI, preferred_element_type=F32)


def dot_nt(a, b):
    return lax.dot_general(a, b, (((1,), (1,)), ((), ())), precision=HI, preferred_element_type=F32)


def system(matrix, target):
    work = jnp.concatenate([0.5 * (matrix + matrix.T), target], axis=1)
    return work * (1.0 / work[0:1, 0:1])


def pivots(work, start, stop):
    n = work.shape[0]
    rows = lax.broadcasted_iota(jnp.int32, (n, 1), 0)
    for k in range(start, stop, 4):
        col = [jnp.broadcast_to(work[:, k + i : k + i + 1], work.shape) for i in range(4)]
        row = [work[k + i : k + i + 1, :] for i in range(4)]

        def at(i, j):
            return col[j][k + i : k + i + 1, :]

        a, b, c = at(0, 0), at(0, 1), at(1, 1)
        e, f, g, h = at(0, 2), at(0, 3), at(1, 2), at(1, 3)
        p, q, s = at(2, 2), at(2, 3), at(3, 3)
        inverse = 1.0 / (a * c - b * b)
        n0, n1 = (c * row[0] - b * row[1]) * inverse, (a * row[1] - b * row[0]) * inverse
        e1, f1 = (c * e - b * g) * inverse, (c * f - b * h) * inverse
        g1, h1 = (a * g - b * e) * inverse, (a * h - b * f) * inverse
        p, q, s = p - (e * e1 + g * g1), q - (e * f1 + g * h1), s - (f * f1 + h * h1)
        r2, r3 = row[2] - (e * n0 + g * n1), row[3] - (f * n0 + h * n1)
        inverse = 1.0 / (p * s - q * q)
        m2, m3 = (s * r2 - q * r3) * inverse, (p * r3 - q * r2) * inverse
        m0, m1 = n0 - (e1 * m2 + f1 * m3), n1 - (g1 * m2 + h1 * m3)
        work = work - (col[0] * m0 + col[1] * m1) - (col[2] * m2 + col[3] * m3)
        for i, solved in enumerate((m0, m1, m2, m3)):
            work = jnp.where(rows == k + i, solved, work)
    return work


def tile_block(x_far, y_far, s_far, x_home, y_home, s_home):
    dx = x_far - x_home
    dy = y_far - y_home
    square = jnp.maximum(dx * dx + dy * dy, 1e-30)
    inverse = lax.rsqrt(square)
    z = square * inverse
    near = ((((-0.25 * z + 0.5) * z + 0.625) * z) - 5.0 / 3.0) * square + 1.0
    rest = jnp.maximum(2.0 - z, 0.0)
    rest2 = rest * rest
    far = rest2 * rest2 * ((z * (1.0 / 12.0) + 1.0 / 6.0) - inverse * (1.0 / 24.0))
    return (s_far * s_home) * jnp.where(z <= 1.0, near, far)


class Exchange:
    def __init__(self, send_sems, recv_sems, base):
        self.send_sems, self.recv_sems, self.base = send_sems, recv_sems, base

    def copy(self, src, dst, index, device):
        return pltpu.make_async_remote_copy(
            src_ref=src,
            dst_ref=dst,
            send_sem=self.send_sems.at[self.base + index],
            recv_sem=self.recv_sems.at[self.base + index],
            device_id=device,
            device_id_type=MESH,
        )


def kernel(
    cfg, v0_ref, geo_ref, err_ref, own_ref, w_ref, r_ref,
    pb, hb, xb, yb, sb, ub0, ub1, cb, acc0, acc1, rs0, rs1, v1_ref, vt, basis,
    l0, t0, y0, z0, g0, l1, t1, y1, z1, g1, l2, t2, y2, z2, g2, send_sems, recv_sems,
):
    R, T, NY, REACH = cfg
    NZ = R // NY
    S = 2 * REACH - 1
    n = v0_ref.shape[0]
    mid = REACH - 1
    r = lax.axis_index("region")
    t = lax.axis_index("tile")
    y = lax.rem(r, NY)
    z = lax.div(r, NY)
    offsets = [d for k in sorted(range(1, REACH), key=lambda k: -min(k, NY - k)) for d in (k, -k)]
    route = {d: via for d, via in RELAY.items() if d in offsets and via in offsets}
    early = [mid] + [mid - d for d in offsets if d not in route]
    late = [mid - d for d in offsets if d in route]
    close = min(2, REACH - 1)

    def region(d):
        return (lax.rem(r + d + R, R), t)

    def along_tile(o):
        return (r, lax.rem(t + o, T))

    def along_y(o):
        return (z * NY + lax.rem(y + o, NY), t)

    def along_z(o):
        return (lax.rem(z + o, NZ) * NY + y, t)

    def farthest_first(count):
        return sorted(range(1, count), key=lambda o: -min(o, count - o))

    peers = [region(d) for d in offsets] + [along_tile(o) for o in range(1, T)]
    peers += [along_y(o) for o in range(1, NY)] + [along_z(o) for o in range(1, NZ)]

    barrier = pltpu.get_barrier_semaphore()
    for peer in peers:
        pl.semaphore_signal(barrier, inc=1, device_id=peer, device_id_type=MESH)

    base = [0]

    def stage(count):
        made = Exchange(send_sems, recv_sems, base[0])
        base[0] += count
        return made

    pb[mid, 0:2, :] = geo_ref[0:2, :] * 2.0
    pb[mid, 2:3, :] = geo_ref[2:3, :]
    pb[mid, 3:4, :] = jnp.zeros((1, LANES), F32)
    pb[mid, 3:4, 0:REACH] = jnp.where(own_ref[0:1, :] >= 0, 1.0, 0.0)
    hb[0] = pb[mid]
    ub0[mid] = v0_ref[...].astype(BF16)
    vt[0, :n] = v0_ref[...]

    start_gram = dot_nt(v0_ref[...], v0_ref[...])
    l0[...] = jnp.concatenate([start_gram, start_gram], axis=1).reshape(l0.shape)

    pl.semaphore_wait(barrier, len(peers))

    class Sum:
        def __init__(self, local, tile_part, y_part, z_part, result):
            self.local, self.parts, self.result = local, (tile_part, y_part, z_part), result
            self.stages = [stage(T - 1), stage(NY - 1), stage(NZ - 1), stage(T - 1)]
            self.pending = []

        def start(self, copies):
            for copy in copies:
                copy.start()
            self.pending = copies
            sends.extend(copies)

        def wait(self):
            for copy in self.pending:
                copy.wait_recv()

        def send_tile(self):
            self.parts[0][t] = self.local[t]
            self.start([
                self.stages[0].copy(self.local.at[lax.rem(t + o, T)], self.parts[0].at[t], o - 1, along_tile(o))
                for o in farthest_first(T)
            ])

        def total(self, part, count):
            self.wait()
            value = part[0]
            for i in range(1, count):
                value = value + part[i]
            return value

        def send_y(self):
            self.parts[1][y] = self.total(self.parts[0], T)
            part = self.parts[1].at[y]
            self.start([self.stages[1].copy(part, part, o - 1, along_y(o)) for o in farthest_first(NY)])

        def send_z(self):
            self.parts[2][z] = self.total(self.parts[1], NY)
            part = self.parts[2].at[z]
            self.start([self.stages[2].copy(part, part, o - 1, along_z(o)) for o in farthest_first(NZ)])

        def send_result(self):
            self.result[t] = self.total(self.parts[2], NZ)
            part = self.result.at[t]
            self.start([self.stages[3].copy(part, part, o - 1, along_tile(o)) for o in farthest_first(T)])

        def finish(self):
            self.wait()
            return self.result[...].reshape(-1, LANES)

    start = Sum(l0, t0, y0, z0, g0)
    first = Sum(l1, t1, y1, z1, g1)
    second = Sum(l2, t2, y2, z2, g2)

    geo_stage, home_stage, u0_stage, begin_stage = stage(len(offsets)), stage(T - 1), stage(len(offsets)), stage(T - 1)
    geo_copies = {d: geo_stage.copy(pb.at[mid], pb.at[mid - d], i, region(d)) for i, d in enumerate(offsets)}
    home_copies = [home_stage.copy(hb.at[0], hb.at[o], o - 1, along_tile(o)) for o in farthest_first(T)]
    u0_copies = [u0_stage.copy(ub0.at[mid], ub0.at[mid - d], i, region(d)) for i, d in enumerate(offsets)]
    begin_copies = [begin_stage.copy(vt.at[0, :n], vt.at[o, :n], o - 1, along_tile(o)) for o in farthest_first(T)]
    sends = [*geo_copies.values(), *home_copies, *u0_copies, *begin_copies]
    for copy in [*geo_copies.values(), *home_copies]:
        copy.start()
    start.send_tile()
    for copy in u0_copies + begin_copies:
        copy.start()

    def spread(s):
        block = pb[s]
        d = s - mid
        listed = pb[mid if d >= 0 else s, 3:4, abs(d) : abs(d) + 1]
        columns = block.T
        xb[s] = jnp.broadcast_to(columns[:, 0:1], (LANES, LANES))
        yb[s] = jnp.broadcast_to(columns[:, 1:2], (LANES, LANES))
        sb[s] = jnp.broadcast_to(columns[:, 2:3] * listed, (LANES, LANES))

    def build(step, carry):
        for o in range(T):
            home = hb[o]
            block = tile_block(xb[step], yb[step], sb[step], home[0:1, :], home[1:2, :], home[2:3, :])
            cb[o, step] = block.astype(BF16)
        return carry

    spread(mid)
    for copy in home_copies:
        copy.wait_recv()
    for d in offsets:
        if abs(d) <= close:
            geo_copies[d].wait_recv()
            spread(mid - d)
    lax.fori_loop(mid - close, mid + close + 1, build, 0)
    for d in offsets:
        if abs(d) > close:
            geo_copies[d].wait_recv()
            spread(mid - d)
    start.send_y()
    lax.fori_loop(0, mid - close, build, 0)
    lax.fori_loop(mid + close + 1, S, build, 0)

    def product(ub, acc, slots, add=False, copies=None):
        slots = sorted(slots)
        whole = jnp.concatenate([ub[s] for s in slots], axis=1)
        runs = []
        for s in slots:
            if runs and runs[-1][1] == s:
                runs[-1][1] = s + 1
            else:
                runs.append([s, s + 1])

        def order(step):
            half = lax.div(step + 1, 2)
            return T // 2 + half - 2 * half * lax.rem(step, 2)

        def chunk(step, carry):
            o = order(step)
            tiles = [cb[o, a:b].reshape((b - a) * LANES, LANES) for a, b in runs]
            tiles = tiles[0] if len(tiles) == 1 else jnp.concatenate(tiles, axis=0)
            value = jnp.dot(whole, tiles, preferred_element_type=F32)
            acc[o] = acc[o] + value if add else value
            if copies is not None:

                @pl.when(step >= 1)
                def _():
                    copies(order(step - 1)).start()

            return carry

        lax.fori_loop(0, T, chunk, 0)

    def scatter(acc, rs):
        found = stage(T - 1)

        def copies(o):
            return found.copy(acc.at[o], rs.at[o - 1], o - 1, (r, lax.rem(t - o + T, T)))

        return copies

    def gathered(acc, rs, copies):
        total = acc[0]
        for o in range(1, T):
            copy = copies(o)
            copy.wait_recv()
            total = total + rs[o - 1]
            sends.append(copy)
        return total

    start.send_z()
    for copy in u0_copies:
        copy.wait_recv()
    scatter0 = scatter(acc0, rs0)
    product(ub0, acc0, list(range(S)), copies=scatter0)
    start.send_result()
    v1_ref[...] = err_ref[...] * v0_ref[...] + gathered(acc0, rs0, scatter0)

    ub1[mid] = v1_ref[...].astype(BF16)
    u1_stage = stage(len(offsets))
    u1_copies = {}
    for i, d in enumerate(offsets):
        via = route.get(d, 0)
        u1_copies[d] = u1_stage.copy(ub1.at[mid - via], ub1.at[mid - d], i, region(d - via))

    for d in offsets:
        if d not in route:
            u1_copies[d].start()
    vt[0, n:] = v1_ref[...]
    both = vt[0]
    l1[...] = dot_nt(v1_ref[...], both).reshape(l1.shape)
    first.send_tile()
    eye = (
        lax.broadcasted_iota(jnp.int32, (n, n), 0) == lax.broadcasted_iota(jnp.int32, (n, n), 1)
    ).astype(F32)
    for d in sorted(set(route.values()), key=abs):
        u1_copies[d].wait_recv()
        for beyond in offsets:
            if route.get(beyond) == d:
                u1_copies[beyond].start()
    sends.extend(u1_copies.values())
    first.send_y()
    basis_stage = stage(T - 1)
    basis_copies = [basis_stage.copy(vt.at[0, n:], vt.at[o, n:], o - 1, along_tile(o)) for o in farthest_first(T)]
    for copy in basis_copies:
        copy.start()
    sends.extend(basis_copies)
    for d in offsets:
        if d not in route and d not in route.values():
            u1_copies[d].wait_recv()
    product(ub1, acc1, early)
    for d in offsets:
        if d in route:
            u1_copies[d].wait_recv()
    if late:
        product(ub1, acc1, late, add=True)
    first.send_z()
    acc1[0] = acc1[0] + err_ref[...] * v1_ref[...]

    for copy in begin_copies + basis_copies:
        copy.wait_recv()
    part = jnp.concatenate([acc1[o] for o in range(T)], axis=1)
    whole = jnp.concatenate([vt[o] for o in range(T)], axis=1)
    l2[...] = dot_nt(part, whole).reshape(l2.shape)
    second.send_tile()
    g00 = start.finish()[:, :n]
    inverse = pivots(system(g00, eye * g00[0:1, 0:1]), 0, n)[:, n:] * (1.0 / g00[0:1, 0:1])
    second.send_y()
    first.send_result()

    gram = first.finish()
    g10, g11 = gram[:, :n], gram[:, n:]
    g01 = g10.T
    scatter1 = scatter(acc1, rs1)
    for o in farthest_first(T):
        scatter1(o).start()
    second.send_z()
    step1 = pivots(system(g01, g00), 0, n)[:, n:]
    next_squares = (g00 - dot_nn(g01, step1)) - dot_nn(step1.T, g10 - dot_nn(g11, step1))
    conjugacy = dot_nn(inverse, next_squares)
    p = jnp.concatenate([eye + conjugacy.T, -step1.T], axis=1)
    second.send_result()
    on_v1 = dot_nn(p, jnp.concatenate([g01, g11], axis=0))
    v0, v1 = v0_ref[...], v1_ref[...]
    basis[:n, :LANES] = v0
    basis[n:, :LANES] = v1
    basis[:n, LANES:] = v1
    basis[n:, LANES:] = gathered(acc1, rs1, scatter1)
    ahead = dot_nn(p, basis[...])
    moved = dot_nn(step1.T, basis[:n, :])
    on_v2 = dot_nt(p, second.finish())
    curvature = dot_nt(jnp.concatenate([on_v1, on_v2], axis=1), p)
    step2 = pivots(system(curvature, next_squares), 0, n)[:, n:].T
    update = dot_nn(step2, ahead)
    w_ref[...] = moved[:, :LANES] + update[:, :LANES]
    r_ref[...] = (v0 - moved[:, LANES:]) - update[:, LANES:]
    for copy in sends:
        copy.wait_send()


def solution(mesh):
    R, T = mesh.shape["region"], mesh.shape["tile"]
    NY = 8 if R % 8 == 0 else 2
    NZ = R // NY

    def shards(innovations, obs_geometry, obs_error, tile_owner):
        n, m = innovations.shape
        reach = tile_owner.shape[1]
        S = 2 * reach - 1
        copies = 3 * 2 * (reach - 1) + 5 * (T - 1) + 3 * (2 * (T - 1) + NY - 1 + NZ - 1)

        def buffer(count, rows):
            return pltpu.VMEM((count, rows, LANES), F32)

        def sum_buffers(h):
            return [buffer(T, h), buffer(T, h), buffer(NY, h), buffer(NZ, h), buffer(T, h)]

        return pl.pallas_call(
            functools.partial(kernel, (R, T, NY, reach)),
            out_shape=[pltpu.VMEM((n, m), F32)] * 2,
            in_specs=[pl.BlockSpec(memory_space=pltpu.VMEM)] * 4,
            out_specs=[pl.BlockSpec(memory_space=pltpu.VMEM)] * 2,
            scratch_shapes=[
                buffer(S, 4), buffer(T, 4),
                buffer(S, LANES), buffer(S, LANES), buffer(S, LANES),
                pltpu.VMEM((S, n, LANES), BF16), pltpu.VMEM((S, n, LANES), BF16),
                pltpu.VMEM((T, S, LANES, LANES), BF16),
                buffer(T, n), buffer(T, n), buffer(T - 1, n), buffer(T - 1, n),
                pltpu.VMEM((n, LANES), F32), buffer(T, 2 * n), pltpu.VMEM((2 * n, 2 * LANES), F32),
                *sum_buffers(n // T), *sum_buffers(n // T), *sum_buffers(n // T),
                pltpu.SemaphoreType.DMA((copies,)), pltpu.SemaphoreType.DMA((copies,)),
            ],
            compiler_params=pltpu.CompilerParams(collective_id=0, has_side_effects=True),
        )(innovations, obs_geometry, obs_error.reshape(1, m), tile_owner)

    return jax.shard_map(
        shards,
        mesh=mesh,
        in_specs=(
            P(None, ("region", "tile")),
            P(None, ("region", "tile")),
            P(("region", "tile")),
            P("region", None),
        ),
        out_specs=(P(None, ("region", "tile")), P(None, ("region", "tile"))),
        check_vma=False,
    )
```

```python
import functools

import jax
import jax.numpy as jnp
from jax import lax
from jax.experimental import pallas as pl
from jax.experimental.pallas import tpu as pltpu
from jax.sharding import PartitionSpec as P

MESH = pl.DeviceIdType.MESH
F32 = jnp.float32
BF16 = jnp.bfloat16
HI = lax.Precision.HIGHEST
LANES = 128
RELAY = {4: 2, -4: -2, 3: 2, -3: -2, 5: 6, -5: -6}


def dot_nn(a, b):
    return lax.dot_general(a, b, (((1,), (0,)), ((), ())), precision=HI, preferred_element_type=F32)


def dot_nt(a, b):
    return lax.dot_general(a, b, (((1,), (1,)), ((), ())), precision=HI, preferred_element_type=F32)


def system(matrix, target):
    work = jnp.concatenate([0.5 * (matrix + matrix.T), target], axis=1)
    return work * (1.0 / work[0:1, 0:1])


def pivots(work, start, stop):
    n = work.shape[0]
    rows = lax.broadcasted_iota(jnp.int32, (n, 1), 0)
    for k in range(start, stop, 4):
        col = [jnp.broadcast_to(work[:, k + i : k + i + 1], work.shape) for i in range(4)]
        row = [work[k + i : k + i + 1, :] for i in range(4)]

        def at(i, j):
            return col[j][k + i : k + i + 1, :]

        a, b, c = at(0, 0), at(0, 1), at(1, 1)
        e, f, g, h = at(0, 2), at(0, 3), at(1, 2), at(1, 3)
        p, q, s = at(2, 2), at(2, 3), at(3, 3)
        inverse = 1.0 / (a * c - b * b)
        n0, n1 = (c * row[0] - b * row[1]) * inverse, (a * row[1] - b * row[0]) * inverse
        e1, f1 = (c * e - b * g) * inverse, (c * f - b * h) * inverse
        g1, h1 = (a * g - b * e) * inverse, (a * h - b * f) * inverse
        p, q, s = p - (e * e1 + g * g1), q - (e * f1 + g * h1), s - (f * f1 + h * h1)
        r2, r3 = row[2] - (e * n0 + g * n1), row[3] - (f * n0 + h * n1)
        inverse = 1.0 / (p * s - q * q)
        m2, m3 = (s * r2 - q * r3) * inverse, (p * r3 - q * r2) * inverse
        m0, m1 = n0 - (e1 * m2 + f1 * m3), n1 - (g1 * m2 + h1 * m3)
        work = work - (col[0] * m0 + col[1] * m1) - (col[2] * m2 + col[3] * m3)
        for i, solved in enumerate((m0, m1, m2, m3)):
            work = jnp.where(rows == k + i, solved, work)
    return work


def tile_block(x_far, y_far, s_far, x_home, y_home, s_home):
    dx = x_far - x_home
    dy = y_far - y_home
    square = jnp.maximum(dx * dx + dy * dy, 1e-30)
    inverse = lax.rsqrt(square)
    z = square * inverse
    near = ((((-0.25 * z + 0.5) * z + 0.625) * z) - 5.0 / 3.0) * square + 1.0
    rest = jnp.maximum(2.0 - z, 0.0)
    rest2 = rest * rest
    far = rest2 * rest2 * ((z * (1.0 / 12.0) + 1.0 / 6.0) - inverse * (1.0 / 24.0))
    return (s_far * s_home) * jnp.where(z <= 1.0, near, far)


class Exchange:
    def __init__(self, send_sems, recv_sems, base):
        self.send_sems, self.recv_sems, self.base = send_sems, recv_sems, base

    def copy(self, src, dst, index, device):
        return pltpu.make_async_remote_copy(
            src_ref=src,
            dst_ref=dst,
            send_sem=self.send_sems.at[self.base + index],
            recv_sem=self.recv_sems.at[self.base + index],
            device_id=device,
            device_id_type=MESH,
        )


def kernel(
    cfg, v0_in, geo_in, err_in, own_in, w_ref, r_ref,
    v0_ref, geo_ref, err_ref, own_ref, in_sems,
    pb, hb, xb, yb, sb, ub0, ub1, cb, acc0, acc1, rs0, rs1, v1_ref, vt, basis,
    l0, t0, y0, z0, g0, l1, t1, y1, z1, g1, l2, t2, y2, z2, g2, send_sems, recv_sems,
):
    R, T, NY, REACH = cfg
    loads = [
        pltpu.make_async_copy(src, dst, in_sems.at[i])
        for i, (src, dst) in enumerate([(geo_in, geo_ref), (own_in, own_ref), (v0_in, v0_ref), (err_in, err_ref)])
    ]
    for copy in loads:
        copy.start()
    NZ = R // NY
    S = 2 * REACH - 1
    n = v0_ref.shape[0]
    mid = REACH - 1
    r = lax.axis_index("region")
    t = lax.axis_index("tile")
    y = lax.rem(r, NY)
    z = lax.div(r, NY)
    offsets = [d for k in sorted(range(1, REACH), key=lambda k: -min(k, NY - k)) for d in (k, -k)]
    route = {d: via for d, via in RELAY.items() if d in offsets and via in offsets}
    early = [mid] + [mid - d for d in offsets if d not in route]
    late = [mid - d for d in offsets if d in route]
    close = min(2, REACH - 1)

    def region(d):
        return (lax.rem(r + d + R, R), t)

    def along_tile(o):
        return (r, lax.rem(t + o, T))

    def along_y(o):
        return (z * NY + lax.rem(y + o, NY), t)

    def along_z(o):
        return (lax.rem(z + o, NZ) * NY + y, t)

    def farthest_first(count):
        return sorted(range(1, count), key=lambda o: -min(o, count - o))

    peers = [region(d) for d in offsets] + [along_tile(o) for o in range(1, T)]
    peers += [along_y(o) for o in range(1, NY)] + [along_z(o) for o in range(1, NZ)]

    barrier = pltpu.get_barrier_semaphore()
    for peer in peers:
        pl.semaphore_signal(barrier, inc=1, device_id=peer, device_id_type=MESH)

    for copy in loads:
        copy.wait()
    base = [0]

    def stage(count):
        made = Exchange(send_sems, recv_sems, base[0])
        base[0] += count
        return made

    pb[mid, 0:2, :] = geo_ref[0:2, :] * 2.0
    pb[mid, 2:3, :] = geo_ref[2:3, :]
    pb[mid, 3:4, :] = jnp.zeros((1, LANES), F32)
    pb[mid, 3:4, 0:REACH] = jnp.where(own_ref[0:1, :] >= 0, 1.0, 0.0)
    hb[0] = pb[mid]
    ub0[mid] = v0_ref[...].astype(BF16)
    vt[0, :n] = v0_ref[...]

    start_gram = dot_nt(v0_ref[...], v0_ref[...])
    l0[...] = jnp.concatenate([start_gram, start_gram], axis=1).reshape(l0.shape)

    pl.semaphore_wait(barrier, len(peers))

    class Sum:
        def __init__(self, local, tile_part, y_part, z_part, result):
            self.local, self.parts, self.result = local, (tile_part, y_part, z_part), result
            self.stages = [stage(T - 1), stage(NY - 1), stage(NZ - 1), stage(T - 1)]
            self.pending = []

        def start(self, copies):
            for copy in copies:
                copy.start()
            self.pending = copies
            sends.extend(copies)

        def wait(self):
            for copy in self.pending:
                copy.wait_recv()

        def send_tile(self):
            self.parts[0][t] = self.local[t]
            self.start([
                self.stages[0].copy(self.local.at[lax.rem(t + o, T)], self.parts[0].at[t], o - 1, along_tile(o))
                for o in farthest_first(T)
            ])

        def total(self, part, count):
            self.wait()
            value = part[0]
            for i in range(1, count):
                value = value + part[i]
            return value

        def send_y(self):
            self.parts[1][y] = self.total(self.parts[0], T)
            part = self.parts[1].at[y]
            self.start([self.stages[1].copy(part, part, o - 1, along_y(o)) for o in farthest_first(NY)])

        def send_z(self):
            self.parts[2][z] = self.total(self.parts[1], NY)
            part = self.parts[2].at[z]
            self.start([self.stages[2].copy(part, part, o - 1, along_z(o)) for o in farthest_first(NZ)])

        def send_result(self):
            self.result[t] = self.total(self.parts[2], NZ)
            part = self.result.at[t]
            self.start([self.stages[3].copy(part, part, o - 1, along_tile(o)) for o in farthest_first(T)])

        def finish(self):
            self.wait()
            return self.result[...].reshape(-1, LANES)

    start = Sum(l0, t0, y0, z0, g0)
    first = Sum(l1, t1, y1, z1, g1)
    second = Sum(l2, t2, y2, z2, g2)

    geo_stage, home_stage, u0_stage, begin_stage = stage(len(offsets)), stage(T - 1), stage(len(offsets)), stage(T - 1)
    geo_copies = {d: geo_stage.copy(pb.at[mid], pb.at[mid - d], i, region(d)) for i, d in enumerate(offsets)}
    home_copies = [home_stage.copy(hb.at[0], hb.at[o], o - 1, along_tile(o)) for o in farthest_first(T)]
    u0_copies = [u0_stage.copy(ub0.at[mid], ub0.at[mid - d], i, region(d)) for i, d in enumerate(offsets)]
    begin_copies = [begin_stage.copy(vt.at[0, :n], vt.at[o, :n], o - 1, along_tile(o)) for o in farthest_first(T)]
    sends = [*geo_copies.values(), *home_copies, *u0_copies, *begin_copies]
    for copy in [*geo_copies.values(), *home_copies]:
        copy.start()
    start.send_tile()
    for copy in u0_copies + begin_copies:
        copy.start()

    def spread(s):
        block = pb[s]
        d = s - mid
        listed = pb[mid if d >= 0 else s, 3:4, abs(d) : abs(d) + 1]
        columns = block.T
        xb[s] = jnp.broadcast_to(columns[:, 0:1], (LANES, LANES))
        yb[s] = jnp.broadcast_to(columns[:, 1:2], (LANES, LANES))
        sb[s] = jnp.broadcast_to(columns[:, 2:3] * listed, (LANES, LANES))

    def build(step, carry):
        for o in range(T):
            home = hb[o]
            block = tile_block(xb[step], yb[step], sb[step], home[0:1, :], home[1:2, :], home[2:3, :])
            cb[o, step] = block.astype(BF16)
        return carry

    spread(mid)
    for copy in home_copies:
        copy.wait_recv()
    for d in offsets:
        if abs(d) <= close:
            geo_copies[d].wait_recv()
            spread(mid - d)
    lax.fori_loop(mid - close, mid + close + 1, build, 0)
    for d in offsets:
        if abs(d) > close:
            geo_copies[d].wait_recv()
            spread(mid - d)
    start.send_y()
    lax.fori_loop(0, mid - close, build, 0)
    lax.fori_loop(mid + close + 1, S, build, 0)

    def product(ub, acc, slots, add=False, copies=None):
        slots = sorted(slots)
        whole = jnp.concatenate([ub[s] for s in slots], axis=1)
        runs = []
        for s in slots:
            if runs and runs[-1][1] == s:
                runs[-1][1] = s + 1
            else:
                runs.append([s, s + 1])

        def order(step):
            half = lax.div(step + 1, 2)
            return T // 2 + half - 2 * half * lax.rem(step, 2)

        def chunk(step, carry):
            o = order(step)
            tiles = [cb[o, a:b].reshape((b - a) * LANES, LANES) for a, b in runs]
            tiles = tiles[0] if len(tiles) == 1 else jnp.concatenate(tiles, axis=0)
            value = jnp.dot(whole, tiles, preferred_element_type=F32)
            acc[o] = acc[o] + value if add else value
            if copies is not None:

                @pl.when(step >= 1)
                def _():
                    copies(order(step - 1)).start()

            return carry

        lax.fori_loop(0, T, chunk, 0)

    def scatter(acc, rs):
        found = stage(T - 1)

        def copies(o):
            return found.copy(acc.at[o], rs.at[o - 1], o - 1, (r, lax.rem(t - o + T, T)))

        return copies

    def gathered(acc, rs, copies):
        total = acc[0]
        for o in range(1, T):
            copy = copies(o)
            copy.wait_recv()
            total = total + rs[o - 1]
            sends.append(copy)
        return total

    start.send_z()
    for copy in u0_copies:
        copy.wait_recv()
    scatter0 = scatter(acc0, rs0)
    product(ub0, acc0, list(range(S)), copies=scatter0)
    start.send_result()
    v1_ref[...] = err_ref[...] * v0_ref[...] + gathered(acc0, rs0, scatter0)

    ub1[mid] = v1_ref[...].astype(BF16)
    u1_stage = stage(len(offsets))
    u1_copies = {}
    for i, d in enumerate(offsets):
        via = route.get(d, 0)
        u1_copies[d] = u1_stage.copy(ub1.at[mid - via], ub1.at[mid - d], i, region(d - via))

    for d in sorted(offsets, key=lambda d: (d not in route.values(), abs(d))):
        if d not in route:
            u1_copies[d].start()
    vt[0, n:] = v1_ref[...]
    both = vt[0]
    l1[...] = dot_nt(v1_ref[...], both).reshape(l1.shape)
    first.send_tile()
    eye = (
        lax.broadcasted_iota(jnp.int32, (n, n), 0) == lax.broadcasted_iota(jnp.int32, (n, n), 1)
    ).astype(F32)
    for d in sorted(set(route.values()), key=abs):
        u1_copies[d].wait_recv()
        for beyond in offsets:
            if route.get(beyond) == d:
                u1_copies[beyond].start()
    sends.extend(u1_copies.values())
    first.send_y()
    basis_stage = stage(T - 1)
    basis_copies = [basis_stage.copy(vt.at[0, n:], vt.at[o, n:], o - 1, along_tile(o)) for o in farthest_first(T)]
    for copy in basis_copies:
        copy.start()
    sends.extend(basis_copies)
    for d in offsets:
        if d not in route and d not in route.values():
            u1_copies[d].wait_recv()
    product(ub1, acc1, early)
    for d in offsets:
        if d in route:
            u1_copies[d].wait_recv()
    if late:
        product(ub1, acc1, late, add=True)
    first.send_z()
    acc1[0] = acc1[0] + err_ref[...] * v1_ref[...]

    for copy in begin_copies + basis_copies:
        copy.wait_recv()
    part = jnp.concatenate([acc1[o] for o in range(T)], axis=1)
    whole = jnp.concatenate([vt[o] for o in range(T)], axis=1)
    l2[...] = dot_nt(part, whole).reshape(l2.shape)
    second.send_tile()
    g00 = start.finish()[:, :n]
    inverse = pivots(system(g00, eye * g00[0:1, 0:1]), 0, n)[:, n:] * (1.0 / g00[0:1, 0:1])
    second.send_y()
    first.send_result()

    gram = first.finish()
    g10, g11 = gram[:, :n], gram[:, n:]
    g01 = g10.T
    scatter1 = scatter(acc1, rs1)
    for o in farthest_first(T):
        scatter1(o).start()
    second.send_z()
    step1 = pivots(system(g01, g00), 0, n)[:, n:]
    next_squares = (g00 - dot_nn(g01, step1)) - dot_nn(step1.T, g10 - dot_nn(g11, step1))
    conjugacy = dot_nn(inverse, next_squares)
    p = jnp.concatenate([eye + conjugacy.T, -step1.T], axis=1)
    second.send_result()
    on_v1 = dot_nn(p, jnp.concatenate([g01, g11], axis=0))
    v0, v1 = v0_ref[...], v1_ref[...]
    basis[:n, :LANES] = v0
    basis[n:, :LANES] = v1
    basis[:n, LANES:] = v1
    basis[n:, LANES:] = gathered(acc1, rs1, scatter1)
    ahead = dot_nn(p, basis[...])
    moved = dot_nn(step1.T, basis[:n, :])
    on_v2 = dot_nt(p, second.finish())
    curvature = dot_nt(jnp.concatenate([on_v1, on_v2], axis=1), p)
    step2 = pivots(system(curvature, next_squares), 0, n)[:, n:].T
    update = dot_nn(step2, ahead)
    w_ref[...] = moved[:, :LANES] + update[:, :LANES]
    r_ref[...] = (v0 - moved[:, LANES:]) - update[:, LANES:]
    for copy in sends:
        copy.wait_send()


def solution(mesh):
    R, T = mesh.shape["region"], mesh.shape["tile"]
    NY = 8 if R % 8 == 0 else 2
    NZ = R // NY

    def shards(innovations, obs_geometry, obs_error, tile_owner):
        n, m = innovations.shape
        reach = tile_owner.shape[1]
        S = 2 * reach - 1
        copies = 3 * 2 * (reach - 1) + 5 * (T - 1) + 3 * (2 * (T - 1) + NY - 1 + NZ - 1)

        def buffer(count, rows):
            return pltpu.VMEM((count, rows, LANES), F32)

        def sum_buffers(h):
            return [buffer(T, h), buffer(T, h), buffer(NY, h), buffer(NZ, h), buffer(T, h)]

        return pl.pallas_call(
            functools.partial(kernel, (R, T, NY, reach)),
            out_shape=[pltpu.VMEM((n, m), F32)] * 2,
            in_specs=[pl.BlockSpec(memory_space=pl.ANY)] * 4,
            out_specs=[pl.BlockSpec(memory_space=pltpu.VMEM)] * 2,
            scratch_shapes=[
                pltpu.VMEM((n, m), F32), pltpu.VMEM((3, m), F32), pltpu.VMEM((1, m), F32),
                pltpu.VMEM((1, reach), jnp.int32), pltpu.SemaphoreType.DMA((4,)),
                buffer(S, 4), buffer(T, 4),
                buffer(S, LANES), buffer(S, LANES), buffer(S, LANES),
                pltpu.VMEM((S, n, LANES), BF16), pltpu.VMEM((S, n, LANES), BF16),
                pltpu.VMEM((T, S, LANES, LANES), BF16),
                buffer(T, n), buffer(T, n), buffer(T - 1, n), buffer(T - 1, n),
                pltpu.VMEM((n, LANES), F32), buffer(T, 2 * n), pltpu.VMEM((2 * n, 2 * LANES), F32),
                *sum_buffers(n // T), *sum_buffers(n // T), *sum_buffers(n // T),
                pltpu.SemaphoreType.DMA((copies,)), pltpu.SemaphoreType.DMA((copies,)),
            ],
            compiler_params=pltpu.CompilerParams(collective_id=0, has_side_effects=True),
        )(innovations, obs_geometry, obs_error.reshape(1, m), tile_owner)

    return jax.shard_map(
        shards,
        mesh=mesh,
        in_specs=(
            P(None, ("region", "tile")),
            P(None, ("region", "tile")),
            P(("region", "tile")),
            P("region", None),
        ),
        out_specs=(P(None, ("region", "tile")), P(None, ("region", "tile"))),
        check_vma=False,
    )
```

```python
import functools

import jax
import jax.numpy as jnp
from jax import lax
from jax.experimental import pallas as pl
from jax.experimental.pallas import tpu as pltpu
from jax.sharding import PartitionSpec as P

MESH = pl.DeviceIdType.MESH
F32 = jnp.float32
BF16 = jnp.bfloat16
HI = lax.Precision.HIGHEST
LANES = 128
RELAY = {4: 2, -4: -2, 3: 2, -3: -2, 5: 6, -5: -6}


def dot_nn(a, b):
    return lax.dot_general(a, b, (((1,), (0,)), ((), ())), precision=HI, preferred_element_type=F32)


def dot_nt(a, b):
    return lax.dot_general(a, b, (((1,), (1,)), ((), ())), precision=HI, preferred_element_type=F32)


def system(matrix, target):
    work = jnp.concatenate([0.5 * (matrix + matrix.T), target], axis=1)
    return work * (1.0 / work[0:1, 0:1])


def pivots(work, start, stop):
    n = work.shape[0]
    rows = lax.broadcasted_iota(jnp.int32, (n, 1), 0)
    for k in range(start, stop, 4):
        col = [jnp.broadcast_to(work[:, k + i : k + i + 1], work.shape) for i in range(4)]
        row = [work[k + i : k + i + 1, :] for i in range(4)]

        def at(i, j):
            return col[j][k + i : k + i + 1, :]

        a, b, c = at(0, 0), at(0, 1), at(1, 1)
        e, f, g, h = at(0, 2), at(0, 3), at(1, 2), at(1, 3)
        p, q, s = at(2, 2), at(2, 3), at(3, 3)
        inverse = 1.0 / (a * c - b * b)
        n0, n1 = (c * row[0] - b * row[1]) * inverse, (a * row[1] - b * row[0]) * inverse
        e1, f1 = (c * e - b * g) * inverse, (c * f - b * h) * inverse
        g1, h1 = (a * g - b * e) * inverse, (a * h - b * f) * inverse
        p, q, s = p - (e * e1 + g * g1), q - (e * f1 + g * h1), s - (f * f1 + h * h1)
        r2, r3 = row[2] - (e * n0 + g * n1), row[3] - (f * n0 + h * n1)
        inverse = 1.0 / (p * s - q * q)
        m2, m3 = (s * r2 - q * r3) * inverse, (p * r3 - q * r2) * inverse
        m0, m1 = n0 - (e1 * m2 + f1 * m3), n1 - (g1 * m2 + h1 * m3)
        work = work - (col[0] * m0 + col[1] * m1) - (col[2] * m2 + col[3] * m3)
        for i, solved in enumerate((m0, m1, m2, m3)):
            work = jnp.where(rows == k + i, solved, work)
    return work


def tile_block(x_far, y_far, s_far, x_home, y_home, s_home):
    dx = x_far - x_home
    dy = y_far - y_home
    square = jnp.maximum(dx * dx + dy * dy, 1e-30)
    inverse = lax.rsqrt(square)
    z = square * inverse
    near = ((((-0.25 * z + 0.5) * z + 0.625) * z) - 5.0 / 3.0) * square + 1.0
    rest = jnp.maximum(2.0 - z, 0.0)
    rest2 = rest * rest
    far = rest2 * rest2 * ((z * (1.0 / 12.0) + 1.0 / 6.0) - inverse * (1.0 / 24.0))
    return (s_far * s_home) * jnp.where(z <= 1.0, near, far)


class Exchange:
    def __init__(self, send_sems, recv_sems, base):
        self.send_sems, self.recv_sems, self.base = send_sems, recv_sems, base

    def copy(self, src, dst, index, device):
        return pltpu.make_async_remote_copy(
            src_ref=src,
            dst_ref=dst,
            send_sem=self.send_sems.at[self.base + index],
            recv_sem=self.recv_sems.at[self.base + index],
            device_id=device,
            device_id_type=MESH,
        )


def kernel(
    cfg, v0_in, geo_in, err_in, own_in, w_ref, r_ref,
    v0_ref, geo_ref, err_ref, own_ref, in_sems,
    pb, hb, xb, yb, sb, ub0, ub1, cb, acc0, acc1, rs0, rs1, v1_ref, vt, basis,
    l0, t0, y0, z0, g0, l1, t1, y1, z1, g1, l2, t2, y2, z2, g2, send_sems, recv_sems,
):
    R, T, NY, REACH = cfg
    loads = [
        pltpu.make_async_copy(src, dst, in_sems.at[i])
        for i, (src, dst) in enumerate([(geo_in, geo_ref), (own_in, own_ref), (v0_in, v0_ref), (err_in, err_ref)])
    ]
    for copy in loads:
        copy.start()
    NZ = R // NY
    S = 2 * REACH - 1
    n = v0_ref.shape[0]
    mid = REACH - 1
    r = lax.axis_index("region")
    t = lax.axis_index("tile")
    y = lax.rem(r, NY)
    z = lax.div(r, NY)
    offsets = [d for k in sorted(range(1, REACH), key=lambda k: -min(k, NY - k)) for d in (k, -k)]
    route = {d: via for d, via in RELAY.items() if d in offsets and via in offsets}
    early = [mid] + [mid - d for d in offsets if d not in route]
    late = [mid - d for d in offsets if d in route]
    close = min(2, REACH - 1)

    def region(d):
        return (lax.rem(r + d + R, R), t)

    def along_tile(o):
        return (r, lax.rem(t + o, T))

    def along_y(o):
        return (z * NY + lax.rem(y + o, NY), t)

    def along_z(o):
        return (lax.rem(z + o, NZ) * NY + y, t)

    def farthest_first(count):
        return sorted(range(1, count), key=lambda o: -min(o, count - o))

    peers = [region(d) for d in offsets] + [along_tile(o) for o in range(1, T)]
    peers += [along_y(o) for o in range(1, NY)] + [along_z(o) for o in range(1, NZ)]

    barrier = pltpu.get_barrier_semaphore()
    for peer in peers:
        pl.semaphore_signal(barrier, inc=1, device_id=peer, device_id_type=MESH)

    for copy in loads:
        copy.wait()
    base = [0]

    def stage(count):
        made = Exchange(send_sems, recv_sems, base[0])
        base[0] += count
        return made

    pb[mid, 0:2, :] = geo_ref[0:2, :] * 2.0
    pb[mid, 2:3, :] = geo_ref[2:3, :]
    pb[mid, 3:4, :] = jnp.zeros((1, LANES), F32)
    pb[mid, 3:4, 0:REACH] = jnp.where(own_ref[0:1, :] >= 0, 1.0, 0.0)
    hb[0] = pb[mid]
    ub0[mid] = v0_ref[...].astype(BF16)
    vt[0, :n] = v0_ref[...]

    start_gram = dot_nt(v0_ref[...], v0_ref[...])
    l0[...] = jnp.concatenate([start_gram, start_gram], axis=1).reshape(l0.shape)

    pl.semaphore_wait(barrier, len(peers))

    class Sum:
        def __init__(self, local, tile_part, y_part, z_part, result):
            self.local, self.parts, self.result = local, (tile_part, y_part, z_part), result
            self.stages = [stage(T - 1), stage(NY - 1), stage(NZ - 1), stage(T - 1)]
            self.pending = []

        def start(self, copies):
            for copy in copies:
                copy.start()
            self.pending = copies
            sends.extend(copies)

        def wait(self):
            for copy in self.pending:
                copy.wait_recv()

        def send_tile(self):
            self.parts[0][t] = self.local[t]
            self.start([
                self.stages[0].copy(self.local.at[lax.rem(t + o, T)], self.parts[0].at[t], o - 1, along_tile(o))
                for o in farthest_first(T)
            ])

        def total(self, part, count):
            self.wait()
            value = part[0]
            for i in range(1, count):
                value = value + part[i]
            return value

        def send_y(self):
            self.parts[1][y] = self.total(self.parts[0], T)
            part = self.parts[1].at[y]
            self.start([self.stages[1].copy(part, part, o - 1, along_y(o)) for o in farthest_first(NY)])

        def send_z(self):
            self.parts[2][z] = self.total(self.parts[1], NY)
            part = self.parts[2].at[z]
            self.start([self.stages[2].copy(part, part, o - 1, along_z(o)) for o in farthest_first(NZ)])

        def send_result(self):
            self.result[t] = self.total(self.parts[2], NZ)
            part = self.result.at[t]
            self.start([self.stages[3].copy(part, part, o - 1, along_tile(o)) for o in farthest_first(T)])

        def finish(self):
            self.wait()
            return self.result[...].reshape(-1, LANES)

    start = Sum(l0, t0, y0, z0, g0)
    first = Sum(l1, t1, y1, z1, g1)
    second = Sum(l2, t2, y2, z2, g2)

    geo_stage, home_stage, u0_stage, begin_stage = stage(len(offsets)), stage(T - 1), stage(len(offsets)), stage(T - 1)
    geo_copies = {d: geo_stage.copy(pb.at[mid], pb.at[mid - d], i, region(d)) for i, d in enumerate(offsets)}
    home_copies = [home_stage.copy(hb.at[0], hb.at[o], o - 1, along_tile(o)) for o in farthest_first(T)]
    u0_copies = [u0_stage.copy(ub0.at[mid], ub0.at[mid - d], i, region(d)) for i, d in enumerate(offsets)]
    begin_copies = [begin_stage.copy(vt.at[0, :n], vt.at[o, :n], o - 1, along_tile(o)) for o in farthest_first(T)]
    sends = [*geo_copies.values(), *home_copies, *u0_copies, *begin_copies]
    for copy in [*geo_copies.values(), *home_copies]:
        copy.start()
    start.send_tile()
    for copy in u0_copies + begin_copies:
        copy.start()

    def spread(s):
        block = pb[s]
        d = s - mid
        listed = pb[mid if d >= 0 else s, 3:4, abs(d) : abs(d) + 1]
        columns = block.T
        xb[s] = jnp.broadcast_to(columns[:, 0:1], (LANES, LANES))
        yb[s] = jnp.broadcast_to(columns[:, 1:2], (LANES, LANES))
        sb[s] = jnp.broadcast_to(columns[:, 2:3] * listed, (LANES, LANES))

    def build(step, carry):
        for o in range(T):
            home = hb[o]
            block = tile_block(xb[step], yb[step], sb[step], home[0:1, :], home[1:2, :], home[2:3, :])
            cb[o // 2, step, :, o % 2 * LANES : (o % 2 + 1) * LANES] = block.astype(BF16)
        return carry

    spread(mid)
    for copy in home_copies:
        copy.wait_recv()
    for d in offsets:
        if abs(d) <= close:
            geo_copies[d].wait_recv()
            spread(mid - d)
    lax.fori_loop(mid - close, mid + close + 1, build, 0)
    for d in offsets:
        if abs(d) > close:
            geo_copies[d].wait_recv()
            spread(mid - d)
    start.send_y()
    lax.fori_loop(0, mid - close, build, 0)
    lax.fori_loop(mid + close + 1, S, build, 0)

    def product(ub, acc, slots, add=False, copies=None):
        slots = sorted(slots)
        whole = jnp.concatenate([ub[s] for s in slots], axis=1)
        runs = []
        for s in slots:
            if runs and runs[-1][1] == s:
                runs[-1][1] = s + 1
            else:
                runs.append([s, s + 1])

        def order(step):
            half = lax.div(step + 1, 2)
            return T // 4 + half - 2 * half * lax.rem(step, 2)

        def chunk(step, carry):
            pair = order(step)
            tiles = [cb[pair, a:b].reshape((b - a) * LANES, 2 * LANES) for a, b in runs]
            tiles = tiles[0] if len(tiles) == 1 else jnp.concatenate(tiles, axis=0)
            value = jnp.dot(whole, tiles, preferred_element_type=F32)
            for i in range(2):
                o, half = 2 * pair + i, value[:, i * LANES : (i + 1) * LANES]
                acc[o] = acc[o] + half if add else half
            if copies is not None:

                @pl.when(step >= 1)
                def _():
                    for i in range(2):
                        copies(2 * order(step - 1) + i).start()

            return carry

        lax.fori_loop(0, T // 2, chunk, 0)
        if copies is not None:
            copies(1).start()

    def scatter(acc, rs):
        found = stage(T - 1)

        def copies(o):
            return found.copy(acc.at[o], rs.at[o - 1], o - 1, (r, lax.rem(t - o + T, T)))

        return copies

    def gathered(acc, rs, copies):
        total = acc[0]
        for o in range(1, T):
            copy = copies(o)
            copy.wait_recv()
            total = total + rs[o - 1]
            sends.append(copy)
        return total

    start.send_z()
    for copy in u0_copies:
        copy.wait_recv()
    scatter0 = scatter(acc0, rs0)
    product(ub0, acc0, list(range(S)), copies=scatter0)
    start.send_result()
    v1_ref[...] = err_ref[...] * v0_ref[...] + gathered(acc0, rs0, scatter0)

    ub1[mid] = v1_ref[...].astype(BF16)
    u1_stage = stage(len(offsets))
    u1_copies = {}
    for i, d in enumerate(offsets):
        via = route.get(d, 0)
        u1_copies[d] = u1_stage.copy(ub1.at[mid - via], ub1.at[mid - d], i, region(d - via))

    for d in sorted(offsets, key=lambda d: (d not in route.values(), abs(d))):
        if d not in route:
            u1_copies[d].start()
    vt[0, n:] = v1_ref[...]
    both = vt[0]
    l1[...] = dot_nt(v1_ref[...], both).reshape(l1.shape)
    first.send_tile()
    eye = (
        lax.broadcasted_iota(jnp.int32, (n, n), 0) == lax.broadcasted_iota(jnp.int32, (n, n), 1)
    ).astype(F32)
    for d in sorted(set(route.values()), key=abs):
        u1_copies[d].wait_recv()
        for beyond in offsets:
            if route.get(beyond) == d:
                u1_copies[beyond].start()
    sends.extend(u1_copies.values())
    first.send_y()
    basis_stage = stage(T - 1)
    basis_copies = [basis_stage.copy(vt.at[0, n:], vt.at[o, n:], o - 1, along_tile(o)) for o in farthest_first(T)]
    for copy in basis_copies:
        copy.start()
    sends.extend(basis_copies)
    for d in offsets:
        if d not in route and d not in route.values():
            u1_copies[d].wait_recv()
    product(ub1, acc1, early)
    for d in offsets:
        if d in route:
            u1_copies[d].wait_recv()
    if late:
        product(ub1, acc1, late, add=True)
    first.send_z()
    acc1[0] = acc1[0] + err_ref[...] * v1_ref[...]

    for copy in begin_copies + basis_copies:
        copy.wait_recv()
    part = jnp.concatenate([acc1[o] for o in range(T)], axis=1)
    whole = jnp.concatenate([vt[o] for o in range(T)], axis=1)
    l2[...] = dot_nt(part, whole).reshape(l2.shape)
    second.send_tile()
    g00 = start.finish()[:, :n]
    inverse = pivots(system(g00, eye * g00[0:1, 0:1]), 0, n)[:, n:] * (1.0 / g00[0:1, 0:1])
    second.send_y()
    first.send_result()

    gram = first.finish()
    g10, g11 = gram[:, :n], gram[:, n:]
    g01 = g10.T
    scatter1 = scatter(acc1, rs1)
    for o in farthest_first(T):
        scatter1(o).start()
    second.send_z()
    step1 = pivots(system(g01, g00), 0, n)[:, n:]
    next_squares = (g00 - dot_nn(g01, step1)) - dot_nn(step1.T, g10 - dot_nn(g11, step1))
    conjugacy = dot_nn(inverse, next_squares)
    p = jnp.concatenate([eye + conjugacy.T, -step1.T], axis=1)
    second.send_result()
    on_v1 = dot_nn(p, jnp.concatenate([g01, g11], axis=0))
    v0, v1 = v0_ref[...], v1_ref[...]
    basis[:n, :LANES] = v0
    basis[n:, :LANES] = v1
    basis[:n, LANES:] = v1
    basis[n:, LANES:] = gathered(acc1, rs1, scatter1)
    ahead = dot_nn(p, basis[...])
    moved = dot_nn(step1.T, basis[:n, :])
    on_v2 = dot_nt(p, second.finish())
    curvature = dot_nt(jnp.concatenate([on_v1, on_v2], axis=1), p)
    step2 = pivots(system(curvature, next_squares), 0, n)[:, n:].T
    update = dot_nn(step2, ahead)
    w_ref[...] = moved[:, :LANES] + update[:, :LANES]
    r_ref[...] = (v0 - moved[:, LANES:]) - update[:, LANES:]
    for copy in sends:
        copy.wait_send()


def solution(mesh):
    R, T = mesh.shape["region"], mesh.shape["tile"]
    NY = 8 if R % 8 == 0 else 2
    NZ = R // NY

    def shards(innovations, obs_geometry, obs_error, tile_owner):
        n, m = innovations.shape
        reach = tile_owner.shape[1]
        S = 2 * reach - 1
        copies = 3 * 2 * (reach - 1) + 5 * (T - 1) + 3 * (2 * (T - 1) + NY - 1 + NZ - 1)

        def buffer(count, rows):
            return pltpu.VMEM((count, rows, LANES), F32)

        def sum_buffers(h):
            return [buffer(T, h), buffer(T, h), buffer(NY, h), buffer(NZ, h), buffer(T, h)]

        return pl.pallas_call(
            functools.partial(kernel, (R, T, NY, reach)),
            out_shape=[pltpu.VMEM((n, m), F32)] * 2,
            in_specs=[pl.BlockSpec(memory_space=pl.ANY)] * 4,
            out_specs=[pl.BlockSpec(memory_space=pltpu.VMEM)] * 2,
            scratch_shapes=[
                pltpu.VMEM((n, m), F32), pltpu.VMEM((3, m), F32), pltpu.VMEM((1, m), F32),
                pltpu.VMEM((1, reach), jnp.int32), pltpu.SemaphoreType.DMA((4,)),
                buffer(S, 4), buffer(T, 4),
                buffer(S, LANES), buffer(S, LANES), buffer(S, LANES),
                pltpu.VMEM((S, n, LANES), BF16), pltpu.VMEM((S, n, LANES), BF16),
                pltpu.VMEM((T // 2, S, LANES, 2 * LANES), BF16),
                buffer(T, n), buffer(T, n), buffer(T - 1, n), buffer(T - 1, n),
                pltpu.VMEM((n, LANES), F32), buffer(T, 2 * n), pltpu.VMEM((2 * n, 2 * LANES), F32),
                *sum_buffers(n // T), *sum_buffers(n // T), *sum_buffers(n // T),
                pltpu.SemaphoreType.DMA((copies,)), pltpu.SemaphoreType.DMA((copies,)),
            ],
            compiler_params=pltpu.CompilerParams(collective_id=0, has_side_effects=True),
        )(innovations, obs_geometry, obs_error.reshape(1, m), tile_owner)

    return jax.shard_map(
        shards,
        mesh=mesh,
        in_specs=(
            P(None, ("region", "tile")),
            P(None, ("region", "tile")),
            P(("region", "tile")),
            P("region", None),
        ),
        out_specs=(P(None, ("region", "tile")), P(None, ("region", "tile"))),
        check_vma=False,
    )
```
